512 devices in a mesh: section: 8 (over z_lo), space: 64 (over y, z_hi, x, core).
Axes of the slice: x: 4, y: 4, z: 16 (z_hi: 2, z_lo: 8; z = z_hi * 8 + z_lo), core: 2. Of those that a mesh axis runs over, the one named last changes fastest.
Arguments:
- acts: bfloat16 [8, 2, 8192, 1024], P('section', None, 'space'), may hold values from -6 to 6
- upstream: bfloat16 [2, 8192, 1024], P(None, 'space'), may hold values from -4 to 4
- weights: bfloat16 [8, 1024, 1024], P('section'), may hold values from -0.1875 to 0.1875
- neighbours: int32 [8192, 6], P('space'), may hold values from 0 to 8191, as said below
Outputs:
- input_grads: bfloat16 [8, 2, 8192, 1024], P('section', None, 'space')
- weight_grads: float32 [8, 1024, 1024], P('section', 'space')
The draws below stay inside these ranges and needn't reach their ends.
Inputs may be any that keep to these rules, and one draw needn't show every extreme that they name: neighbours[i, k] is a node at most 32 positions from node i along the node order, taken cyclically over all 8192 nodes; the distance 32 is reached on both sides.
All inputs are finite; a program needn't handle non-finite values.
Results may differ from the reference program's by a relative error of at most 0.014.
Values may be sent and summed in bfloat16 or wider, within the bound.
No kernel may reach another device: no remote copies, remote signals or barrier semaphores. Data moves between devices by JAX's collectives and lax.ppermute only.
A program may use at most 64 MiB of HBM per device.

```python
import jax
import jax.numpy as jnp
from jax import lax

D = 1024
K = 6
HALO = 32
M = 2
SECTIONS = 8
NODES = 8192


def draw_neighbours(key, part):
    offsets = jax.random.randint(key, (NODES, K), -HALO, HALO + 1)
    offsets = offsets.at[0, 0].set(HALO).at[1, 0].set(-HALO)
    base = jnp.arange(NODES, dtype=jnp.int32)[:, None]
    return jnp.mod(base + offsets, NODES).astype(jnp.int32)


def shard_levels(key, dims, split, smallest, largest):
    factor_of = 1.0
    for dim, blocks in split:
        draws = jax.random.uniform(jax.random.fold_in(jax.random.fold_in(key, 6), dim), (blocks,), jnp.float32, smallest / len(split), largest / len(split))
        factor_of = factor_of * jnp.repeat(jnp.exp(draws), dims[dim] // blocks).reshape((-1,) + (1,) * (len(dims) - 1 - dim))
    return factor_of


def bell_draw(rng, dims, width, limit, shards=(), held_as=jnp.bfloat16):
    loudness = shard_levels(rng, dims, shards, -0.22, 0.18) if shards else 1.0
    values = jax.random.normal(rng, dims, jnp.float32) * width * loudness
    return jnp.minimum(jnp.maximum(values, -limit), limit).astype(held_as)


def setup_inputs(seed: int = 0) -> dict:
    seeds = jax.random.split(jax.random.key(seed), 5)
    acts = bell_draw(seeds[0], (SECTIONS, M, NODES, D), 1.0, 6.0, ((0, 8), (2, 64)))
    upstream = bell_draw(seeds[1], (M, NODES, D), 0.5, 4.0, ((1, 64),))
    weights = bell_draw(seeds[2], (SECTIONS, D, D), D ** -0.5, 0.1875, ((0, 8),))
    neighbours = draw_neighbours(jax.random.fold_in(seeds[4], 71), 0)
    return dict(acts=acts, upstream=upstream, weights=weights, neighbours=neighbours)


def layer_back(h_field, g_field, weight, neighbours):
    agg = jnp.mean(h_field[neighbours].astype(jnp.float32), axis=1)
    z_field = (h_field.astype(jnp.float32) + agg).astype(jnp.bfloat16)
    u_field = jnp.dot(z_field, weight, preferred_element_type=jnp.float32)
    sig = jax.nn.sigmoid(u_field)
    du_field = (g_field.astype(jnp.float32) * sig * (1.0 + u_field * (1.0 - sig))).astype(jnp.bfloat16)
    dz_field = lax.dot_general(du_field, weight, (((1,), (1,)), ((), ())), preferred_element_type=jnp.float32)
    share = dz_field * (1.0 / K)
    spread = jnp.zeros(dz_field.shape, jnp.float32).at[neighbours.reshape(-1)].add(
        jnp.broadcast_to(share[:, None, :], (share.shape[0], K, share.shape[1])).reshape(-1, share.shape[1]))
    d_input = (g_field.astype(jnp.float32) + dz_field + spread).astype(jnp.bfloat16)
    d_weight = lax.dot_general(z_field, du_field, (((0,), (0,)), ((), ())), preferred_element_type=jnp.float32)
    return d_input, d_weight


def reference(acts, upstream, weights, neighbours):
    grads = [None] * SECTIONS
    wgrads = [None] * SECTIONS
    carried = [upstream[m] for m in range(M)]
    for section in reversed(range(SECTIONS)):
        total = jnp.zeros((D, D), jnp.float32)
        outs = []
        for m in range(M):
            d_input, d_weight = layer_back(acts[section, m], carried[m], weights[section], neighbours)
            outs.append(d_input)
            total = total + d_weight
        carried = outs
        grads[section] = jnp.stack(outs)
        wgrads[section] = total
    return jnp.stack(grads), jnp.stack(wgrads)
```

```python
import functools

import jax
import jax.numpy as jnp
from jax import lax
from jax.experimental import pallas as pl
from jax.experimental.pallas import tpu as pltpu
from jax.sharding import PartitionSpec as P

K = 6
HALO = 32
EDGE = 2 * HALO
WIDE = 3 * HALO
AXES = ("section", "space")

bf16 = jnp.bfloat16
f32 = jnp.float32
ANY = pl.BlockSpec(memory_space=pl.ANY)
SMEM = pl.BlockSpec(memory_space=pltpu.SMEM)


def copy_all(sems, *jobs):
    copies = [pltpu.make_async_copy(src, dst, sems.at[i]) for i, (src, dst) in enumerate(jobs)]
    for copy in copies:
        copy.start()
    return copies


def transpose_kernel(w_ref, out_ref):
    out_ref[...] = w_ref[...].T


def prepare_kernel(
    flags, h, off, tx, ty, rx, ry, w, factor, mix, z_out, held, off_held, w_held, sems
):
    micro, rows, width = h.shape
    span = rows + 2 * EDGE
    reach = rows + 2 * WIDE
    w_copy = pltpu.make_async_copy(w, w_held, sems.at[0])
    w_copy.start()
    own = copy_all(sems.at[pl.ds(1, micro)], *[(h.at[m], held.at[m, pl.ds(WIDE, rows)]) for m in range(micro)])

    def fetch(low, high):
        jobs = []
        for m in range(micro):
            jobs.append((low.at[pl.ds(m * WIDE, WIDE)], held.at[m, pl.ds(0, WIDE)]))
            jobs.append((high.at[pl.ds(m * WIDE, WIDE)], held.at[m, pl.ds(WIDE + rows, WIDE)]))
        jobs.append((low.at[pl.ds(micro * WIDE, 16)], off_held.at[0]))
        jobs.append((high.at[pl.ds(micro * WIDE, 16)], off_held.at[1]))
        return [pltpu.make_async_copy(s, d, sems.at[1 + micro + i]) for i, (s, d) in enumerate(jobs)]

    for top in (0, 1):
        for even in (0, 1):
            x, y = (tx, ty) if top else (rx, ry)

            @pl.when(jnp.logical_and(flags[7] == top, flags[8] == even))
            def _(x=x, y=y, even=even):
                for copy in fetch(*((y, x) if even else (x, y))):
                    copy.start()

    held[:, reach:, :] = jnp.zeros((micro, held.shape[1] - reach, width), bf16)
    for copy in fetch(tx, ty):
        copy.wait()
    low = [off_held[0, :, 128 * p : 128 * p + 128] for p in range(EDGE // 16)]
    high = [off_held[1, :, 128 * p : 128 * p + 128] for p in range(EDGE // 16)]
    steps = jnp.concatenate([*low, off[...], *high], axis=0).astype(f32)
    lanes = held.shape[1]
    column = lax.broadcasted_iota(jnp.int32, (span, lanes), 1).astype(f32)
    row = lax.broadcasted_iota(jnp.int32, (span, lanes), 0).astype(f32)
    distance = column - row - float(HALO)
    count = jnp.zeros((span, lanes), f32)
    for k in range(K):
        count = count + jnp.where(distance == steps[:, k : k + 1], 1.0, 0.0)
    gather = count.astype(bf16)
    mix[...] = (count + jnp.where(distance == 0.0, float(K), 0.0)).T[:reach].astype(bf16)
    for copy in own:
        copy.wait()
    z_fields = []
    for m in range(micro):
        agg = jnp.dot(gather, held[m], preferred_element_type=f32) * (1.0 / K)
        z_field = (held[m, HALO : HALO + span, :].astype(f32) + agg).astype(bf16)
        z_out[m] = z_field[EDGE : EDGE + rows]
        z_fields.append(z_field)
    w_copy.wait()
    for m in range(micro):
        u = jnp.dot(z_fields[m], w_held[...], preferred_element_type=f32)
        sig = 1.0 / (1.0 + jnp.exp(-u))
        factor[m] = sig * (1.0 + u * (1.0 - sig))


def layer_kernel(layer, m, wide, sources, *refs):
    flags = refs[0]
    g_in = refs[1 : 1 + sources]
    factor, mix, w_t = refs[1 + sources : 4 + sources]
    outs = refs[6 + sources : -7]
    grads, kept = outs[:2]
    sends = outs[2:]
    g_held, f_held, mix_held, w_held, own, du_held, sems = refs[-7:]
    rows = own.shape[0]

    @pl.when(flags[layer] == 1)
    def _():
        even = flags[8] == 1
        mix_copy, f_copy, w_copy = copy_all(
            sems.at[pl.ds(0, 3)], (mix, mix_held), (factor.at[m], f_held), (w_t, w_held)
        )
        low, high = g_held.at[pl.ds(0, EDGE)], g_held.at[pl.ds(EDGE + rows, EDGE)]
        if not wide:
            whole = copy_all(sems.at[pl.ds(3, 1)], (g_in[0], g_held.at[pl.ds(HALO, rows + EDGE)]))
            g_held[:HALO, :] = jnp.zeros((HALO, g_held.shape[1]), bf16)
            g_held[EDGE + rows + HALO :, :] = jnp.zeros((HALO, g_held.shape[1]), bf16)
        else:
            if sources == 3 and layer == 7:
                parts = [g_in[0].at[m]] + [
                    r.at[pl.ds(2 * WIDE + 16 + EDGE * m, EDGE)] for r in g_in[1:]
                ]
            else:
                parts = list(g_in)
            whole = copy_all(sems.at[pl.ds(3, 1)], (parts[0], g_held.at[pl.ds(EDGE, rows)]))

            @pl.when(even)
            def _():
                copy_all(sems.at[pl.ds(4, 2)], (parts[1], high), (parts[2], low))

            @pl.when(jnp.logical_not(even))
            def _():
                copy_all(sems.at[pl.ds(4, 2)], (parts[1], low), (parts[2], high))

            whole = whole + [
                pltpu.make_async_copy(parts[1], low, sems.at[4]),
                pltpu.make_async_copy(parts[2], high, sems.at[5]),
            ]
        f_copy.wait()
        for copy in whole:
            copy.wait()
        du = (g_held[...].astype(f32) * f_held[...]).astype(bf16)
        du_held[...] = du[EDGE : EDGE + rows]
        keep = copy_all(sems.at[pl.ds(6, 1)], (du_held, kept.at[m]))
        mix_copy.wait()
        margin = EDGE if wide else WIDE
        size = rows + EDGE if wide else rows
        mixed = jnp.dot(mix_held[margin : margin + size, :], du, preferred_element_type=f32)
        mixed = (mixed * (1.0 / K)).astype(bf16)
        w_copy.wait()
        dz = jnp.dot(mixed, w_held[...], preferred_element_type=f32)
        first = margin - HALO
        total = (g_held[first : first + size, :].astype(f32) + dz).astype(bf16)
        if wide:
            own[...] = total[HALO : HALO + rows]
            sends[0][...] = total
        else:
            own[...] = total
            if sends:
                sends[0][...] = total

                @pl.when(even)
                def _():
                    sends[1][...] = total[rows - EDGE :]
                    sends[2][...] = total[:EDGE]

                @pl.when(jnp.logical_not(even))
                def _():
                    sends[1][...] = total[:EDGE]
                    sends[2][...] = total[rows - EDGE :]

        save = copy_all(sems.at[pl.ds(7, 1)], (own, grads.at[m]))
        for copy in keep + save:
            copy.wait()


def split_kernel(flags, z, mine, other):
    width = z.shape[-1]
    z_t = z[...].reshape(-1, width).T
    parts = z_t.reshape(width // 32, 2, 16, z_t.shape[1])

    @pl.when(flags[8] == 1)
    def _():
        mine[...] = parts[:, 0].reshape(mine.shape)
        other[...] = parts[:, 1].reshape(other.shape)

    @pl.when(flags[8] == 0)
    def _():
        mine[...] = parts[:, 1].reshape(mine.shape)
        other[...] = parts[:, 0].reshape(other.shape)


def weight_kernel(za, zb, da, db, out):
    total = jnp.dot(za[...], da[...], preferred_element_type=f32)
    total = total + jnp.dot(zb[...], db[...], preferred_element_type=f32)
    out[...] = total.astype(bf16).reshape(out.shape)


def sum_kernel(parts, out):
    total = parts[0].astype(f32)
    for i in range(1, parts.shape[0]):
        total = total + parts[i].astype(f32)
    out[...] = total


def shards(acts, upstream, weights, neighbours):
    sections = lax.axis_size("section")
    count = lax.axis_size("space")
    section = lax.axis_index("section")
    shard = lax.axis_index("space")
    rows = neighbours.shape[0]
    width = weights.shape[2]
    micro = upstream.shape[0]
    nodes = rows * count
    h, w = acts[0], weights[0]
    span = rows + 2 * EDGE
    reach = rows + 2 * WIDE

    even = shard % 2 == 0
    flags = jnp.concatenate(
        [(section == jnp.arange(sections)).astype(jnp.int32), even.astype(jnp.int32)[None]]
    )

    def beside(which, j):
        return (j ^ 1) if which == 0 else (j - 1 if j % 2 == 0 else j + 1) % count

    def edges(which, senders, step):
        return [
            (s * count + j, (s - step) * count + beside(which, j)) for s in senders for j in range(count)
        ]

    def ahead(s):
        return [(s * count + j, (s - 1) * count + j) for j in range(count)]

    ids = shard * rows + jnp.arange(rows, dtype=jnp.int32)[:, None]
    off = jnp.mod(neighbours - ids + nodes // 2, nodes) - nodes // 2
    off = jnp.pad(off.astype(bf16), ((0, 0), (0, 128 - K)))

    def pack(upper):
        def cut(value, size, dim):
            return lax.dynamic_slice_in_dim(value, jnp.where(upper, rows - size, 0), size, dim)

        steps = cut(off, EDGE, 0).reshape(EDGE // 16, 16, 128).transpose(1, 0, 2)
        steps = jnp.pad(steps.reshape(16, -1), ((0, 0), (0, width - 128 * (EDGE // 16))))
        return (
            cut(h, WIDE, 1).reshape(-1, width),
            steps,
            cut(upstream, EDGE, 1).reshape(-1, width),
        )

    pack_x, pack_y = pack(even), pack(jnp.logical_not(even))
    top = [sections - 1]
    rest = list(range(sections - 1))
    ty = lax.ppermute(jnp.concatenate(pack_y), AXES, edges(1, top, 0))
    tx = lax.ppermute(jnp.concatenate(pack_x), AXES, edges(0, top, 0))
    ry = lax.ppermute(jnp.concatenate(pack_y[:2]), AXES, edges(1, rest, 0))
    rx = lax.ppermute(jnp.concatenate(pack_x[:2]), AXES, edges(0, rest, 0))

    w_t = pl.pallas_call(
        transpose_kernel, out_shape=jax.ShapeDtypeStruct((width, width), bf16), name="turn"
    )(w)
    factor, mix, z = pl.pallas_call(
        prepare_kernel,
        out_shape=(
            jax.ShapeDtypeStruct((micro, span, width), f32),
            jax.ShapeDtypeStruct((reach, span), bf16),
            jax.ShapeDtypeStruct((micro, rows, width), bf16),
        ),
        in_specs=[SMEM, ANY, pl.BlockSpec(memory_space=pltpu.VMEM)] + [ANY] * 5,
        scratch_shapes=[
            pltpu.VMEM((micro, -(-reach // 128) * 128, width), bf16),
            pltpu.VMEM((2, 16, width), bf16),
            pltpu.VMEM((width, width), bf16),
            pltpu.SemaphoreType.DMA((3 + 3 * micro,)),
        ],
        name="prepare",
    )(flags, h, off, tx, ty, rx, ry, w)

    grads = jnp.zeros((micro, rows, width), bf16)
    kept = jnp.zeros((micro, rows, width), bf16)
    own_shape = jax.ShapeDtypeStruct((micro, rows, width), bf16)
    received = [[upstream, tx, ty]] * micro
    for layer in reversed(range(sections)):
        wide = layer % 2 == 1
        if layer == 0:
            send_shapes = ()
        elif wide:
            send_shapes = (jax.ShapeDtypeStruct((rows + EDGE, width), bf16),)
        else:
            send_shapes = tuple(jax.ShapeDtypeStruct((r, width), bf16) for r in (rows, EDGE, EDGE))
        arriving = []
        for m in range(micro):
            g_in = received[m]
            n = len(g_in)
            outs = pl.pallas_call(
                functools.partial(layer_kernel, layer, m, wide, n),
                out_shape=(own_shape, own_shape, *send_shapes),
                in_specs=[SMEM] + [ANY] * (n + 5),
                out_specs=[ANY, ANY] + [pl.BlockSpec(memory_space=pltpu.VMEM)] * len(send_shapes),
                input_output_aliases={n + 4: 0, n + 5: 1},
                scratch_shapes=[
                    pltpu.VMEM((span, width), bf16),
                    pltpu.VMEM((span, width), f32),
                    pltpu.VMEM((reach, span), bf16),
                    pltpu.VMEM((width, width), bf16),
                    pltpu.VMEM((rows, width), bf16),
                    pltpu.VMEM((rows, width), bf16),
                    pltpu.SemaphoreType.DMA((8,)),
                ],
                name=f"layer{layer}_{m}",
            )(flags, *g_in, factor, mix, w_t, grads, kept)
            grads, kept, *sends = outs
            if len(sends) == 1:
                arriving.append([lax.ppermute(sends[0], AXES, ahead(layer))])
            elif sends:
                y = lax.ppermute(sends[2], AXES, edges(1, [layer], 1))
                main = lax.ppermute(sends[0], AXES, ahead(layer))
                x = lax.ppermute(sends[1], AXES, edges(0, [layer], 1))
                arriving.append([main, x, y])
        received = arriving

    half = width // 2
    half_shape = jax.ShapeDtypeStruct((half, micro * rows), bf16)
    mine, other = pl.pallas_call(
        split_kernel,
        out_shape=(half_shape, half_shape),
        in_specs=[SMEM, pl.BlockSpec(memory_space=pltpu.VMEM)],
        name="split",
    )(flags, z)
    swap = [(s * count + j, s * count + (j ^ 1)) for s in range(sections) for j in range(count)]
    other = lax.ppermute(other, AXES, swap)
    du = kept.reshape(micro * rows, width)
    du_other = lax.ppermute(du, AXES, swap)
    partial = pl.pallas_call(
        weight_kernel,
        out_shape=jax.ShapeDtypeStruct((count // 2, width // count, width), bf16),
        name="weight",
    )(mine, other, du, du_other)
    groups = [[2 * q + c for q in range(count // 2)] for c in range(2)]
    parts = lax.all_to_all(partial, "space", 0, 0, axis_index_groups=groups)
    weight_grad = pl.pallas_call(
        sum_kernel, out_shape=jax.ShapeDtypeStruct((width // count, width), f32), name="total"
    )(parts)
    return (grads[None], weight_grad[None])


def solution(mesh):
    in_specs = (
        P("section", None, "space", None),
        P(None, "space", None),
        P("section", None, None),
        P("space", None),
    )
    out_specs = (P("section", None, "space", None), P("section", "space", None))
    return jax.shard_map(shards, mesh=mesh, in_specs=in_specs, out_specs=out_specs, check_vma=False)
```

```python
import functools

import jax
import jax.numpy as jnp
from jax import lax
from jax.experimental import pallas as pl
from jax.experimental.pallas import tpu as pltpu
from jax.sharding import PartitionSpec as P


K = 6
HALO = 32
EDGE = 2 * HALO
AXES = ("section", "space")

bf16 = jnp.bfloat16
f32 = jnp.float32
VMEM = pl.BlockSpec(memory_space=pltpu.VMEM)
SMEM = pl.BlockSpec(memory_space=pltpu.SMEM)
LIMIT = pltpu.CompilerParams(vmem_limit_bytes=16 * 1024 * 1024)
EVEN, NEAR, FAR, LOWER, BASE, NODES = 8, 9, 10, 11, 12, 13


def on_chip(value):
    return pltpu.with_memory_space_constraint(value, pltpu.VMEM)


def permute(value, pairs):
    return lax.ppermute(value, AXES, pairs)


def call(kernel, outs, flags, arrays, aliases=None):
    return pl.pallas_call(
        kernel,
        out_shape=tuple(pltpu.VMEM(shape, dtype) for shape, dtype in outs),
        in_specs=[SMEM] + [VMEM] * len(arrays),
        out_specs=tuple([VMEM] * len(outs)),
        input_output_aliases=aliases or {},
        compiler_params=LIMIT,
    )(flags, *[on_chip(a) for a in arrays])


def turn_kernel(flags, w, out):
    out[...] = w[...].T


def pack_kernel(flags, h, up, neighbours, off, *edges):
    micro, rows, width = h.shape
    nodes = flags[NODES]
    even = flags[EVEN] == 1
    ids = flags[BASE] + lax.broadcasted_iota(jnp.int32, neighbours.shape, 0)
    step = neighbours[...] - ids
    step = jnp.where(step > HALO, step - nodes, step)
    step = jnp.where(step < -HALO, step + nodes, step)
    off[...] = jnp.zeros(off.shape, bf16)
    off[:, :K] = step.astype(f32).astype(bf16)
    blank = jnp.zeros((16, width - 256), bf16)

    def edge(upper):
        def cut(value, size):
            return value[rows - size :] if upper else value[:size]

        steps = cut(off, HALO)
        steps = jnp.concatenate([steps[:16], steps[16:], blank], axis=1)
        inner = [cut(h[m], EDGE) for m in range(micro)] + [steps]
        return jnp.concatenate(inner + [cut(up[m], HALO) for m in range(micro)], axis=0)

    lower, upper = edge(False), edge(True)
    x, y = jnp.where(even, upper, lower), jnp.where(even, lower, upper)
    for value, full, short in ((x, edges[0], edges[2]), (y, edges[1], edges[3])):
        full[...] = value
        short[...] = value[: short.shape[0]]


def prepare_kernel(active, flags, h, off, w, from_x, from_y, *refs):
    factor, mix, z_out = refs[-3:]
    micro, rows, _ = h.shape
    span = rows + 2 * HALO
    reach = rows + 2 * EDGE

    @pl.when(flags[active] == 1)
    def _():
        even = flags[EVEN] == 1

        def both(start, size):
            x, y = from_x[start : start + size, :], from_y[start : start + size, :]
            return jnp.where(even, y, x), jnp.where(even, x, y)

        low, high = both(micro * EDGE, 16)
        steps = jnp.concatenate(
            [low[:, :128], low[:, 128:256], off[...], high[:, :128], high[:, 128:256]], axis=0
        ).astype(f32)
        column = lax.broadcasted_iota(jnp.int32, (span, reach), 1).astype(f32)
        row = lax.broadcasted_iota(jnp.int32, (span, reach), 0).astype(f32)
        distance = column - row - float(HALO)
        count = jnp.zeros((span, reach), f32)
        for k in range(K):
            count = count + jnp.where(distance == steps[:, k : k + 1], 1.0, 0.0)
        gather = count.astype(bf16)
        spread = (count + jnp.where(distance == 0.0, float(K), 0.0)).T
        mix[...] = spread[EDGE : EDGE + rows].astype(bf16)
        for m in range(micro):
            low, high = both(m * EDGE, EDGE)
            field = jnp.concatenate([low, h[m], high], axis=0)
            agg = jnp.dot(gather, field, preferred_element_type=f32) * (1.0 / K)
            z_field = (field[HALO : HALO + span].astype(f32) + agg).astype(bf16)
            z_out[m] = z_field[HALO : HALO + rows]
            u = jnp.dot(z_field, w[...], preferred_element_type=f32)
            sig = 1.0 / (1.0 + jnp.exp(-u))
            factor[m] = sig * (1.0 + u * (1.0 - sig))


def layer_kernel(layer, m, fresh, flags, main, from_x, from_y, factor, mix, w_t, *refs):
    grads, kept, *sends = refs[0 if fresh else 2 :]
    micro, rows, _ = grads.shape

    @pl.when(flags[layer] == 1)
    def _():
        even = flags[EVEN] == 1
        if layer == 7:
            start = micro * EDGE + 16 + HALO * m
            own = main[m]
            x, y = (r[start : start + HALO, :] for r in (from_x, from_y))
        else:
            own, x, y = main[...], from_x[...], from_y[...]
        g_field = jnp.concatenate([jnp.where(even, y, x), own, jnp.where(even, x, y)], axis=0)
        du = (g_field.astype(f32) * factor[m]).astype(bf16)
        kept[m] = du[HALO : HALO + rows]
        mixed = jnp.dot(mix[...], du, preferred_element_type=f32)
        mixed = (mixed * (1.0 / K)).astype(bf16)
        dz = jnp.dot(mixed, w_t[...], preferred_element_type=f32)
        total = (own.astype(f32) + dz).astype(bf16)
        grads[m] = total
        if sends:
            upper, lower = total[rows - HALO :], total[:HALO]
            sends[0][...] = total
            sends[1][...] = jnp.where(even, upper, lower)
            sends[2][...] = jnp.where(even, lower, upper)


def split_kernel(flags, z, mine, other):
    micro, rows, width = z.shape
    z_t = z[...].reshape(micro * rows, width).T
    even = flags[EVEN] == 1
    for q in range(width // 32):
        a, b = z_t[32 * q : 32 * q + 16], z_t[32 * q + 16 : 32 * q + 32]
        mine[16 * q : 16 * q + 16, :] = jnp.where(even, a, b)
        other[16 * q : 16 * q + 16, :] = jnp.where(even, b, a)


def weight_kernel(flags, za, zb, da, db, out):
    micro, rows, width = da.shape
    total = jnp.dot(za[...], da[...].reshape(micro * rows, width), preferred_element_type=f32)
    total = total + jnp.dot(
        zb[...], db[...].reshape(micro * rows, width), preferred_element_type=f32
    )
    total = total.astype(bf16)
    for q in range(2 * out.shape[0]):
        y, z_hi, x = q // 8, (q // 4) % 2, q % 4
        out[4 * y + x, 16 * z_hi : 16 * z_hi + 16, :] = total[16 * q : 16 * q + 16]


def sum_kernel(flags, parts, mine, other):
    total = parts[0].astype(f32)
    for i in range(1, parts.shape[0]):
        total = total + parts[i].astype(f32)
    first = flags[LOWER] == 0
    a, b = total[:16], total[16:]
    mine[...] = jnp.where(first, a, b)
    other[...] = jnp.where(first, b, a)


def add_kernel(flags, a, b, out):
    out[...] = a[...] + b[...]


def shards(acts, upstream, weights, neighbours):
    sections = lax.axis_size("section")
    count = lax.axis_size("space")
    section = lax.axis_index("section")
    shard = lax.axis_index("space")
    rows = neighbours.shape[0]
    width = weights.shape[2]
    micro = upstream.shape[0]
    nodes = rows * count
    h, w = acts[0], weights[0]
    span = rows + 2 * HALO
    top = [sections - 1]
    near = [sections - 2, sections - 3]
    rest = list(range(sections - 3))

    near_by = jnp.logical_and(section >= near[-1], section < top[0])
    extra = [shard % 2 == 0, near_by, section < near[-1], (shard // 8) % 2 == 1]
    extra = jnp.stack([*(e.astype(jnp.int32) for e in extra), shard * rows, jnp.int32(nodes)])
    flags = jnp.concatenate([(section == jnp.arange(sections)).astype(jnp.int32), extra])

    def beside(which, j):
        return (j ^ 1) if which == 0 else (j - 1 if j % 2 == 0 else j + 1) % count

    def edges(which, senders, step):
        return [
            (s * count + j, (s - step) * count + beside(which, j)) for s in senders for j in range(count)
        ]

    def ahead(s):
        return [(s * count + j, (s - 1) * count + j) for j in range(count)]

    def swap(bit):
        return [(s * count + j, s * count + (j ^ bit)) for s in range(sections) for j in range(count)]

    short = ((micro * EDGE + 16, width), bf16)
    long = ((micro * (EDGE + HALO) + 16, width), bf16)
    off, tx, ty, x_pack, y_pack = call(
        pack_kernel,
        [((rows, 128), bf16), long, long, short, short],
        flags,
        [h, upstream, neighbours],
    )
    ty = permute(ty, edges(1, top, 0))
    tx = permute(tx, edges(0, top, 0))
    (w_t,) = call(turn_kernel, [((width, width), bf16)], flags, [w])
    field = ((micro, rows, width), bf16)
    made = [((micro, span, width), f32), ((rows, span), bf16), field]

    def prepare(active, sides, old=()):
        return call(
            functools.partial(prepare_kernel, active),
            made,
            flags,
            [h, off, w, *sides, *old],
            {6 + i: i for i in range(len(old))},
        )

    factor, mix, z = prepare(top[0], (tx, ty))

    grads = kept = None
    received = [[upstream, tx, ty]] * micro
    for layer in reversed(range(sections)):
        if layer in (near[0], near[-1]):
            _, active, group = ("near", NEAR, near) if layer == near[0] else ("rest", FAR, rest)
            x_pack, y_pack, factor, grads = lax.optimization_barrier((x_pack, y_pack, factor, grads))
            from_y = permute(y_pack, edges(1, group, 0))
            from_x = permute(x_pack, edges(0, group, 0))
            factor, mix, z = prepare(active, (from_x, from_y), (factor, mix, z))
        if layer == near[-1]:
            half_shape = ((width // 2, micro * rows), bf16)
            mine, other = call(split_kernel, [half_shape] * 2, flags, [z])
            other = permute(other, swap(1))
            grads, other = lax.optimization_barrier((grads, other))
        arriving = []
        for m in range(micro):
            fresh = grads is None
            sent = [((r, width), bf16) for r in (rows, HALO, HALO)] if layer else []
            grads, kept, *sends = call(
                functools.partial(layer_kernel, layer, m, fresh),
                [field, field, *sent],
                flags,
                [*received[m], factor, mix, w_t, *([] if fresh else [grads, kept])],
                {} if fresh else {7: 0, 8: 1},
            )
            if layer:
                y = permute(sends[2], edges(1, [layer], 1))
                main = permute(sends[0], ahead(layer))
                x = permute(sends[1], edges(0, [layer], 1))
                arriving.append([main, x, y])
        received = arriving

    du_other = permute(kept, swap(1))
    (partial,) = call(
        weight_kernel,
        [((count // 4, 2 * width // count, width), bf16)],
        flags,
        [mine, other, kept, du_other],
    )
    groups = [
        [16 * y + 8 * z + 2 * x + c for y in range(4) for x in range(4)]
        for z in range(2)
        for c in range(2)
    ]
    parts = lax.all_to_all(partial, "space", 0, 0, axis_index_groups=groups)
    slab = ((width // count, width), f32)
    mine, other = call(sum_kernel, [slab, slab], flags, [parts])
    other = permute(other, swap(8))
    (weight_grad,) = call(add_kernel, [slab], flags, [mine, other])
    return (grads[None], weight_grad[None])


def solution(mesh):
    in_specs = (
        P("section", None, "space", None),
        P(None, "space", None),
        P("section", None, None),
        P("space", None),
    )
    out_specs = (P("section", None, "space", None), P("section", "space", None))

    return jax.shard_map(shards, mesh=mesh, in_specs=in_specs, out_specs=out_specs, check_vma=False)
```

```python
import functools

import jax
import jax.numpy as jnp
from jax import lax
from jax.experimental import pallas as pl
from jax.experimental.pallas import tpu as pltpu
from jax.sharding import PartitionSpec as P


K = 6
HALO = 32
EDGE = 2 * HALO
WIDE = 3 * HALO
AXES = ("section", "space")

bf16 = jnp.bfloat16
f32 = jnp.float32
VMEM = pl.BlockSpec(memory_space=pltpu.VMEM)
SMEM = pl.BlockSpec(memory_space=pltpu.SMEM)
LIMIT = pltpu.CompilerParams(vmem_limit_bytes=16 * 1024 * 1024)
EVEN, REST, LOWER, BASE, NODES = 8, 9, 10, 11, 12


def on_chip(value):
    return pltpu.with_memory_space_constraint(value, pltpu.VMEM)


def permute(value, pairs):
    return lax.ppermute(value, AXES, pairs)


def call(kernel, outs, flags, arrays, aliases=None):
    return pl.pallas_call(
        kernel,
        out_shape=tuple(pltpu.VMEM(shape, dtype) for shape, dtype in outs),
        in_specs=[SMEM] + [VMEM] * len(arrays),
        out_specs=tuple([VMEM] * len(outs)),
        input_output_aliases=aliases or {},
        compiler_params=LIMIT,
    )(flags, *[on_chip(a) for a in arrays])


def turn_kernel(flags, w, out):
    out[...] = w[...].T


def pack_kernel(flags, h, up, neighbours, off, *edges):
    micro, rows, width = h.shape
    nodes = flags[NODES]
    even = flags[EVEN] == 1
    ids = flags[BASE] + lax.broadcasted_iota(jnp.int32, neighbours.shape, 0)
    step = neighbours[...] - ids
    step = jnp.where(step > HALO, step - nodes, step)
    step = jnp.where(step < -HALO, step + nodes, step)
    off[...] = jnp.zeros(off.shape, bf16)
    off[:, :K] = step.astype(f32).astype(bf16)
    blank = jnp.zeros((16, width - 512), bf16)

    def edge(upper):
        def cut(value, size):
            return value[rows - size :] if upper else value[:size]

        steps = cut(off, EDGE)
        steps = jnp.concatenate([*[steps[16 * p : 16 * p + 16] for p in range(4)], blank], axis=1)
        inner = [cut(h[m], WIDE) for m in range(micro)] + [steps]
        return jnp.concatenate(inner + [cut(up[m], EDGE) for m in range(micro)], axis=0)

    lower, upper = edge(False), edge(True)
    x, y = jnp.where(even, upper, lower), jnp.where(even, lower, upper)
    for value, full, short in ((x, edges[0], edges[2]), (y, edges[1], edges[3])):
        full[...] = value
        short[...] = value[: short.shape[0]]


def slope(u):
    sig = 1.0 / (1.0 + jnp.exp(-u))
    return sig * (1.0 + u * (1.0 - sig))


def prepare_kernel(active, flags, h, off, w, from_x, from_y, *refs):
    factor, mix, z_out = refs[-3:]
    micro, rows, width = h.shape
    span = rows + 2 * EDGE
    reach = rows + 2 * WIDE
    lanes = -(-reach // 128) * 128

    @pl.when(flags[active] == 1)
    def _():
        even = flags[EVEN] == 1

        def both(start, size):
            x, y = from_x[start : start + size, :], from_y[start : start + size, :]
            return jnp.where(even, y, x), jnp.where(even, x, y)

        low, high = both(micro * WIDE, 16)
        cut = [slice(128 * p, 128 * p + 128) for p in range(EDGE // 16)]
        steps = jnp.concatenate(
            [*[low[:, c] for c in cut], off[...], *[high[:, c] for c in cut]], axis=0
        ).astype(f32)
        column = lax.broadcasted_iota(jnp.int32, (span, lanes), 1).astype(f32)
        row = lax.broadcasted_iota(jnp.int32, (span, lanes), 0).astype(f32)
        distance = column - row - float(HALO)
        count = jnp.zeros((span, lanes), f32)
        for k in range(K):
            count = count + jnp.where(distance == steps[:, k : k + 1], 1.0, 0.0)
        gather = count.astype(bf16)
        mix[...] = (count + jnp.where(distance == 0.0, float(K), 0.0)).T[:reach].astype(bf16)
        blank = jnp.zeros((lanes - reach, width), bf16)
        for m in range(micro):
            low, high = both(m * WIDE, WIDE)
            field = jnp.concatenate([low, h[m], high, blank], axis=0)
            agg = jnp.dot(gather, field, preferred_element_type=f32) * (1.0 / K)
            z_field = (field[HALO : HALO + span].astype(f32) + agg).astype(bf16)
            z_out[m] = z_field[EDGE : EDGE + rows]
            factor[m] = slope(jnp.dot(z_field, w[...], preferred_element_type=f32))


def layer_kernel(layer, m, sources, olds, flags, *refs):
    g_in = refs[:sources]
    factor, mix, w_t = refs[sources : sources + 3]
    grads, kept, *sends = refs[sources + 3 + olds :]
    micro, rows, width = grads.shape
    span = rows + EDGE
    odd = layer % 2 == 1

    @pl.when(flags[layer] == 1)
    def _():
        if layer == 7:
            start = micro * WIDE + 16 + EDGE * m
            x, y = (r[start : start + EDGE, :] for r in g_in[1:])
            own, edge = g_in[0][m], jnp.where(flags[EVEN] == 1, x, y)
        else:
            own, edge = g_in[0][...], g_in[1][...]
        g_field = jnp.concatenate([own, edge] if odd else [edge, own], axis=0)
        first = EDGE if odd else HALO
        du = (g_field.astype(f32) * factor[m, first : first + span, :]).astype(bf16)
        kept[m] = du[EDGE - first : EDGE - first + rows]
        blank = [jnp.zeros((n, width), bf16) for n in (first, mix.shape[1] - span - first)]
        parts = [p for p in (blank[0], du, blank[1]) if p.shape[0]]
        above = WIDE + (HALO if odd else 0)
        mixed = jnp.dot(
            mix[above : above + rows, :], jnp.concatenate(parts, axis=0), preferred_element_type=f32
        )
        mixed = (mixed * (1.0 / K)).astype(bf16)
        dz = jnp.dot(mixed, w_t[...], preferred_element_type=f32)
        total = (g_field[HALO : HALO + rows].astype(f32) + dz).astype(bf16)
        grads[m] = total
        if sends:
            sends[0][...] = total
            sends[1][...] = total[rows - EDGE :] if odd else total[:EDGE]


def rim_kernel(flags, grads, out):
    out[...] = grads[:, grads.shape[1] - HALO :, :]


def shift_kernel(flags, grads, rim, out):
    micro, rows, _ = grads.shape
    odd = flags[1] + flags[3] + flags[5] + flags[7] == 1
    for m in range(micro):
        moved = jnp.concatenate([rim[m], grads[m, : rows - HALO, :]], axis=0)
        out[m] = jnp.where(odd, moved, grads[m])


def split_kernel(flags, z, mine, other):
    micro, rows, width = z.shape
    z_t = z[...].reshape(micro * rows, width).T
    even = flags[EVEN] == 1
    for q in range(width // 32):
        a, b = z_t[32 * q : 32 * q + 16], z_t[32 * q + 16 : 32 * q + 32]
        mine[16 * q : 16 * q + 16, :] = jnp.where(even, a, b)
        other[16 * q : 16 * q + 16, :] = jnp.where(even, b, a)


def weight_kernel(flags, za, zb, da, db, out):
    micro, rows, width = da.shape
    total = jnp.dot(za[...], da[...].reshape(micro * rows, width), preferred_element_type=f32)
    total = total + jnp.dot(
        zb[...], db[...].reshape(micro * rows, width), preferred_element_type=f32
    )
    total = total.astype(bf16)
    for q in range(2 * out.shape[0]):
        y, z_hi, x = q // 8, (q // 4) % 2, q % 4
        out[4 * y + x, 16 * z_hi : 16 * z_hi + 16, :] = total[16 * q : 16 * q + 16]


def sum_kernel(flags, parts, mine, other):
    total = parts[0].astype(f32)
    for i in range(1, parts.shape[0]):
        total = total + parts[i].astype(f32)
    first = flags[LOWER] == 0
    a, b = total[:16], total[16:]
    mine[...] = jnp.where(first, a, b)
    other[...] = jnp.where(first, b, a)


def add_kernel(flags, a, b, out):
    out[...] = a[...] + b[...]


def shards(acts, upstream, weights, neighbours):
    sections = lax.axis_size("section")
    count = lax.axis_size("space")
    section = lax.axis_index("section")
    shard = lax.axis_index("space")
    rows = neighbours.shape[0]
    width = weights.shape[2]
    micro = upstream.shape[0]
    nodes = rows * count
    h, w = acts[0], weights[0]
    span = rows + 2 * EDGE
    reach = rows + 2 * WIDE
    top = [sections - 1]
    rest = list(range(sections - 1))

    extra = [shard % 2 == 0, section < top[0]]
    extra.append((shard // 8) % 2 == 1)
    extra = jnp.stack([*(e.astype(jnp.int32) for e in extra), shard * rows, jnp.int32(nodes)])
    flags = jnp.concatenate([(section == jnp.arange(sections)).astype(jnp.int32), extra])

    def beside(which, j):
        return (j ^ 1) if which == 0 else (j - 1 if j % 2 == 0 else j + 1) % count

    def edges(which, senders, step):
        return [
            (s * count + j, (s - step) * count + beside(which, j)) for s in senders for j in range(count)
        ]

    def toward(senders, step, side):
        return [(s * count + j, (s - step) * count + (j + side) % count) for s in senders for j in range(count)]

    def swap(bit):
        return [(s * count + j, s * count + (j ^ bit)) for s in range(sections) for j in range(count)]

    short = ((micro * WIDE + 16, width), bf16)
    long = ((micro * (WIDE + EDGE) + 16, width), bf16)
    off, tx, ty, x_pack, y_pack = call(
        pack_kernel,
        [((rows, 128), bf16), long, long, short, short],
        flags,
        [h, upstream, neighbours],
    )
    ty = permute(ty, edges(1, top, 0))
    tx = permute(tx, edges(0, top, 0))
    (w_t,) = call(turn_kernel, [((width, width), bf16)], flags, [w])
    field = ((micro, rows, width), bf16)
    made = [((micro, span, width), f32), ((reach, span), bf16), field]

    def prepare(active, sides, old=()):
        return call(
            functools.partial(prepare_kernel, active),
            made,
            flags,
            [h, off, w, *sides, *old],
            {6 + i: i for i in range(len(old))},
        )

    prepared = prepare(top[0], (tx, ty))
    grads = kept = None
    received = [[upstream, tx, ty]] * micro
    for layer in reversed(range(sections)):
        if layer == rest[-1]:
            x_pack, y_pack, grads, *prepared = lax.optimization_barrier(
                (x_pack, y_pack, grads, *prepared)
            )
            ry = permute(y_pack, edges(1, rest, 0))
            rx = permute(x_pack, edges(0, rest, 0))
            prepared = prepare(REST, (rx, ry), prepared)
        if layer == rest[-1] - 1:
            half_shape = ((width // 2, micro * rows), bf16)
            grads, z = lax.optimization_barrier((grads, prepared[2]))
            mine, other = call(split_kernel, [half_shape] * 2, flags, [z])
            other = permute(other, swap(1))
            grads, other = lax.optimization_barrier((grads, other))
        factor, mix, _ = prepared
        arriving = []
        for m in range(micro):
            old = [] if grads is None else [grads, kept]
            sent = [((r, width), bf16) for r in (rows, EDGE)] if layer else []
            first = 4 + len(received[m])
            grads, kept, *sends = call(
                functools.partial(layer_kernel, layer, m, len(received[m]), len(old)),
                [field, field, *sent],
                flags,
                [*received[m], factor, mix, w_t, *old],
                {first + i: i for i in range(len(old))},
            )
            if layer:
                side = 1 if layer % 2 else -1
                edge = permute(sends[1], toward([layer], 1, side))
                main = permute(sends[0], toward([layer], 1, 0))
                arriving.append([main, edge])
        received = arriving
        if layer == 1:
            (rim,) = call(rim_kernel, [((micro, HALO, width), bf16)], flags, [grads])
            rim = permute(rim, toward(range(1, sections, 2), 0, 1))

    du_other = permute(kept, swap(1))
    (partial,) = call(
        weight_kernel,
        [((count // 4, 2 * width // count, width), bf16)],
        flags,
        [mine, other, kept, du_other],
    )
    groups = [
        [16 * y + 8 * z + 2 * x + c for y in range(4) for x in range(4)]
        for z in range(2)
        for c in range(2)
    ]
    parts = lax.all_to_all(partial, "space", 0, 0, axis_index_groups=groups)
    slab = ((width // count, width), f32)
    mine, other = call(sum_kernel, [slab, slab], flags, [parts])
    other = permute(other, swap(8))
    (weight_grad,) = call(add_kernel, [slab], flags, [mine, other])
    (grads,) = call(shift_kernel, [field], flags, [grads, rim])
    return (grads[None], weight_grad[None])


def solution(mesh):
    in_specs = (
        P("section", None, "space", None),
        P(None, "space", None),
        P("section", None, None),
        P("space", None),
    )
    out_specs = (P("section", None, "space", None), P("section", "space", None))

    return jax.shard_map(shards, mesh=mesh, in_specs=in_specs, out_specs=out_specs, check_vma=False)
```

```python
import functools

import jax
import jax.numpy as jnp
from jax import lax
from jax.experimental import pallas as pl
from jax.experimental.pallas import tpu as pltpu
from jax.sharding import PartitionSpec as P


K = 6
HALO = 32
EDGE = 2 * HALO
WIDE = 3 * HALO
AXES = ("section", "space")

bf16 = jnp.bfloat16
f32 = jnp.float32
VMEM = pl.BlockSpec(memory_space=pltpu.VMEM)
SMEM = pl.BlockSpec(memory_space=pltpu.SMEM)
LIMIT = pltpu.CompilerParams(vmem_limit_bytes=16 * 1024 * 1024)
EVEN, REST, LOWER, BASE, NODES = 8, 9, 10, 11, 12


def on_chip(value):
    return pltpu.with_memory_space_constraint(value, pltpu.VMEM)


def permute(value, pairs):
    return lax.ppermute(value, AXES, pairs)


def call(kernel, outs, flags, arrays, aliases=None):
    return pl.pallas_call(
        kernel,
        out_shape=tuple(pltpu.VMEM(shape, dtype) for shape, dtype in outs),
        in_specs=[SMEM] + [VMEM] * len(arrays),
        out_specs=tuple([VMEM] * len(outs)),
        input_output_aliases=aliases or {},
        compiler_params=LIMIT,
    )(flags, *[on_chip(a) for a in arrays])


def turn_kernel(flags, w, out):
    out[...] = w[...].T


def pack_kernel(flags, h_ref, up_ref, neighbours, off, *rest):
    *edges, h, up, sems = rest
    micro, rows, width = h.shape
    copies = [
        pltpu.make_async_copy(h_ref, h, sems.at[0]),
        pltpu.make_async_copy(up_ref, up, sems.at[1]),
    ]
    for copy in copies:
        copy.start()
    nodes = flags[NODES]
    even = flags[EVEN] == 1
    ids = flags[BASE] + lax.broadcasted_iota(jnp.int32, neighbours.shape, 0)
    step = neighbours[...] - ids
    step = jnp.where(step > HALO, step - nodes, step)
    step = jnp.where(step < -HALO, step + nodes, step)
    off[...] = jnp.zeros(off.shape, bf16)
    off[:, :K] = step.astype(f32).astype(bf16)
    for copy in copies:
        copy.wait()
    blank = jnp.zeros((16, width - 512), bf16)

    def edge(upper):
        def cut(value, size):
            return value[rows - size :] if upper else value[:size]

        steps = cut(off, EDGE)
        steps = jnp.concatenate([*[steps[16 * p : 16 * p + 16] for p in range(4)], blank], axis=1)
        inner = [cut(h[m], WIDE) for m in range(micro)] + [steps]
        return jnp.concatenate(inner + [cut(up[m], EDGE) for m in range(micro)], axis=0)

    lower, upper = edge(False), edge(True)
    x, y = jnp.where(even, upper, lower), jnp.where(even, lower, upper)
    edges[0][...] = x
    edges[1][...] = y
    edges[2][...] = y[: edges[2].shape[0]]


def slope(u):
    sig = 1.0 / (1.0 + jnp.exp(-u))
    return sig * (1.0 + u * (1.0 - sig))


def prepare_kernel(active, flags, h, off, w, from_x, from_y, *refs):
    factor, mix, z_out = refs[-3:]
    micro, rows, width = h.shape
    span = rows + 2 * EDGE
    reach = rows + 2 * WIDE
    lanes = -(-reach // 128) * 128

    @pl.when(flags[active] == 1)
    def _():
        even = flags[EVEN] == 1

        def both(start, size):
            x, y = from_x[start : start + size, :], from_y[start : start + size, :]
            return jnp.where(even, y, x), jnp.where(even, x, y)

        low, high = both(micro * WIDE, 16)
        cut = [slice(128 * p, 128 * p + 128) for p in range(EDGE // 16)]
        steps = jnp.concatenate(
            [*[low[:, c] for c in cut], off[...], *[high[:, c] for c in cut]], axis=0
        ).astype(f32)
        column = lax.broadcasted_iota(jnp.int32, (span, lanes), 1).astype(f32)
        row = lax.broadcasted_iota(jnp.int32, (span, lanes), 0).astype(f32)
        distance = column - row - float(HALO)
        count = jnp.zeros((span, lanes), f32)
        for k in range(K):
            count = count + jnp.where(distance == steps[:, k : k + 1], 1.0, 0.0)
        gather = count.astype(bf16)
        mix[...] = (count + jnp.where(distance == 0.0, float(K), 0.0)).T[:reach].astype(bf16)
        blank = jnp.zeros((lanes - reach, width), bf16)
        for m in range(micro):
            low, high = both(m * WIDE, WIDE)
            field = jnp.concatenate([low, h[m], high, blank], axis=0)
            agg = jnp.dot(gather, field, preferred_element_type=f32) * (1.0 / K)
            z_field = (field[HALO : HALO + span].astype(f32) + agg).astype(bf16)
            z_out[m] = z_field[EDGE : EDGE + rows]
            factor[m] = slope(jnp.dot(z_field, w[...], preferred_element_type=f32))


def layer_kernel(layer, m, sources, olds, flags, *refs):
    g_in = refs[:sources]
    factor, mix, w_t = refs[sources : sources + 3]
    grads, kept, *sends = refs[sources + 3 + olds :]
    micro, rows, width = grads.shape
    span = rows + EDGE
    odd = layer % 2 == 1

    @pl.when(flags[layer] == 1)
    def _():
        if layer == 7:
            start = micro * WIDE + 16 + EDGE * m
            x, y = (r[start : start + EDGE, :] for r in g_in[1:])
            own, edge = g_in[0][m], jnp.where(flags[EVEN] == 1, x, y)
        else:
            own, edge = g_in[0][...], g_in[1][...]
        g_field = jnp.concatenate([own, edge] if odd else [edge, own], axis=0)
        first = EDGE if odd else HALO
        du = (g_field.astype(f32) * factor[m, first : first + span, :]).astype(bf16)
        kept[m] = du[EDGE - first : EDGE - first + rows]
        blank = [jnp.zeros((n, width), bf16) for n in (first, mix.shape[1] - span - first)]
        parts = [p for p in (blank[0], du, blank[1]) if p.shape[0]]
        above = WIDE + (HALO if odd else 0)
        mixed = jnp.dot(
            mix[above : above + rows, :], jnp.concatenate(parts, axis=0), preferred_element_type=f32
        )
        mixed = (mixed * (1.0 / K)).astype(bf16)
        dz = jnp.dot(mixed, w_t[...], preferred_element_type=f32)
        total = (g_field[HALO : HALO + rows].astype(f32) + dz).astype(bf16)
        grads[m] = total
        if sends:
            sends[0][...] = total
            sends[1][...] = total[rows - EDGE :] if odd else total[:EDGE]


def rim_kernel(flags, grads, out):
    out[...] = grads[:, grads.shape[1] - HALO :, :]


def shift_kernel(flags, grads, rim, out):
    micro, rows, _ = grads.shape
    odd = flags[1] + flags[3] + flags[5] + flags[7] == 1
    for m in range(micro):
        moved = jnp.concatenate([rim[m], grads[m, : rows - HALO, :]], axis=0)
        out[m] = jnp.where(odd, moved, grads[m])


def split_kernel(flags, z, mine, other):
    micro, rows, width = z.shape
    z_t = z[...].reshape(micro * rows, width).T
    even = flags[EVEN] == 1
    for q in range(width // 32):
        a, b = z_t[32 * q : 32 * q + 16], z_t[32 * q + 16 : 32 * q + 32]
        mine[16 * q : 16 * q + 16, :] = jnp.where(even, a, b)
        other[16 * q : 16 * q + 16, :] = jnp.where(even, b, a)


def weight_kernel(flags, za, zb, da, db, far, near):
    micro, rows, width = da.shape
    total = jnp.dot(za[...], da[...].reshape(micro * rows, width), preferred_element_type=f32)
    total = total + jnp.dot(
        zb[...], db[...].reshape(micro * rows, width), preferred_element_type=f32
    )
    total = total.astype(bf16)
    upper = flags[LOWER] == 1
    for y in range(4):
        for x in range(4):
            a, b = (total[16 * q : 16 * q + 16] for q in (8 * y + x, 8 * y + 4 + x))
            far[4 * y + x] = jnp.where(upper, a, b)
            near[4 * y + x] = jnp.where(upper, b, a)


def sum_kernel(flags, parts, out):
    total = parts[0].astype(f32)
    for i in range(1, parts.shape[0]):
        total = total + parts[i].astype(f32)
    out[...] = total


def add_kernel(flags, parts, other, out):
    total = parts[0].astype(f32)
    for i in range(1, parts.shape[0]):
        total = total + parts[i].astype(f32)
    out[...] = total + other[...]


def shards(acts, upstream, weights, neighbours):
    sections = lax.axis_size("section")
    count = lax.axis_size("space")
    section = lax.axis_index("section")
    shard = lax.axis_index("space")
    rows = neighbours.shape[0]
    width = weights.shape[2]
    micro = upstream.shape[0]
    nodes = rows * count
    h, w = acts[0], weights[0]
    span = rows + 2 * EDGE
    reach = rows + 2 * WIDE
    top = [sections - 1]
    rest = list(range(sections - 1))

    extra = [shard % 2 == 0, section < top[0]]
    extra.append((shard // 8) % 2 == 1)
    extra = jnp.stack([*(e.astype(jnp.int32) for e in extra), shard * rows, jnp.int32(nodes)])
    flags = jnp.concatenate([(section == jnp.arange(sections)).astype(jnp.int32), extra])

    def beside(which, j):
        return (j ^ 1) if which == 0 else (j - 1 if j % 2 == 0 else j + 1) % count

    def edges(which, senders, step):
        return [
            (s * count + j, (s - step) * count + beside(which, j)) for s in senders for j in range(count)
        ]

    def toward(senders, step, side):
        return [(s * count + j, (s - step) * count + (j + side) % count) for s in senders for j in range(count)]

    def swap(bit):
        return [(s * count + j, s * count + (j ^ bit)) for s in range(sections) for j in range(count)]

    short = ((micro * WIDE + 16, width), bf16)
    long = ((micro * (WIDE + EDGE) + 16, width), bf16)
    shapes = [((rows, 128), bf16), long, long, short]
    whole = pl.BlockSpec(memory_space=pltpu.HBM)
    off, from_x, ty, y_pack = pl.pallas_call(
        pack_kernel,
        out_shape=tuple(pltpu.VMEM(shape, dtype) for shape, dtype in shapes),
        in_specs=[SMEM, whole, whole, VMEM],
        out_specs=tuple([VMEM] * len(shapes)),
        scratch_shapes=[
            pltpu.VMEM((micro, rows, width), bf16),
            pltpu.VMEM((micro, rows, width), bf16),
            pltpu.SemaphoreType.DMA((2,)),
        ],
        compiler_params=LIMIT,
        name="pack",
    )(flags, *(pltpu.with_memory_space_constraint(a, pltpu.HBM) for a in (h, upstream)), on_chip(neighbours))
    h, upstream, off = lax.optimization_barrier((h, upstream, off))
    ty = permute(ty, edges(1, top, 0))
    from_x = permute(from_x, swap(1))
    (w_t,) = call(turn_kernel, [((width, width), bf16)], flags, [w])
    field = ((micro, rows, width), bf16)
    made = [((micro, span, width), f32), ((reach, span), bf16), field]

    def prepare(active, sides, old=()):
        return call(
            functools.partial(prepare_kernel, active),
            made,
            flags,
            [h, off, w, *sides, *old],
            {6 + i: i for i in range(len(old))},
        )

    prepared = prepare(top[0], (from_x, ty))
    grads = kept = None
    received = [[upstream, from_x, ty]] * micro
    for layer in reversed(range(sections)):
        if layer == rest[-1]:
            y_pack, grads, *prepared = lax.optimization_barrier((y_pack, grads, *prepared))
            ry = permute(y_pack, edges(1, rest, 0))
            prepared = prepare(REST, (from_x, ry), prepared)
        if layer == rest[-1] - 1:
            half_shape = ((width // 2, micro * rows), bf16)
            grads, z = lax.optimization_barrier((grads, prepared[2]))
            mine, other = call(split_kernel, [half_shape] * 2, flags, [z])
            other = permute(other, swap(1))
            grads, other = lax.optimization_barrier((grads, other))
        factor, mix, _ = prepared
        arriving = []
        for m in range(micro):
            old = [] if grads is None else [grads, kept]
            sent = [((r, width), bf16) for r in (rows, EDGE)] if layer else []
            first = 4 + len(received[m])
            grads, kept, *sends = call(
                functools.partial(layer_kernel, layer, m, len(received[m]), len(old)),
                [field, field, *sent],
                flags,
                [*received[m], factor, mix, w_t, *old],
                {first + i: i for i in range(len(old))},
            )
            if layer:
                side = 1 if layer % 2 else -1
                edge = permute(sends[1], toward([layer], 1, side))
                main = permute(sends[0], toward([layer], 1, 0))
                arriving.append([main, edge])
        received = arriving
        if layer == 1:
            (rim,) = call(rim_kernel, [((micro, HALO, width), bf16)], flags, [grads])
            rim = permute(rim, toward(range(1, sections, 2), 0, 1))

    du_other = permute(kept, swap(1))
    slab = (width // count, width)
    far, close = call(
        weight_kernel, [((16, *slab), bf16)] * 2, flags, [mine, other, kept, du_other]
    )
    groups = [
        [16 * y + 8 * z + 2 * x + c for y in range(4) for x in range(4)]
        for z in range(2)
        for c in range(2)
    ]
    far = lax.all_to_all(far, "space", 0, 0, axis_index_groups=groups)
    close = lax.all_to_all(close, "space", 0, 0, axis_index_groups=groups)
    (far,) = call(sum_kernel, [(slab, f32)], flags, [far])
    other = permute(far, swap(8))
    (weight_grad,) = call(add_kernel, [(slab, f32)], flags, [close, other])
    (grads,) = call(shift_kernel, [field], flags, [grads, rim])
    return (grads[None], weight_grad[None])


def solution(mesh):
    in_specs = (
        P("section", None, "space", None),
        P(None, "space", None),
        P("section", None, None),
        P("space", None),
    )
    out_specs = (P("section", None, "space", None), P("section", "space", None))

    return jax.shard_map(shards, mesh=mesh, in_specs=in_specs, out_specs=out_specs, check_vma=False)
```

```python
import functools

import jax
import jax.numpy as jnp
from jax import lax
from jax.experimental import pallas as pl
from jax.experimental.pallas import tpu as pltpu
from jax.sharding import PartitionSpec as P


K = 6
HALO = 32
EDGE = 2 * HALO
WIDE = 3 * HALO
AXES = ("section", "space")

bf16 = jnp.bfloat16
f32 = jnp.float32
VMEM = pl.BlockSpec(memory_space=pltpu.VMEM)
SMEM = pl.BlockSpec(memory_space=pltpu.SMEM)
LIMIT = pltpu.CompilerParams(vmem_limit_bytes=16 * 1024 * 1024)
EVEN, REST, LOWER, BASE, NODES = 8, 9, 10, 11, 12


def on_chip(value):
    return pltpu.with_memory_space_constraint(value, pltpu.VMEM)


def permute(value, pairs):
    return lax.ppermute(value, AXES, pairs)


def call(kernel, outs, flags, arrays, aliases=None):
    return pl.pallas_call(
        kernel,
        out_shape=tuple(pltpu.VMEM(shape, dtype) for shape, dtype in outs),
        in_specs=[SMEM] + [VMEM] * len(arrays),
        out_specs=tuple([VMEM] * len(outs)),
        input_output_aliases=aliases or {},
        compiler_params=LIMIT,
    )(flags, *[on_chip(a) for a in arrays])


def turn_kernel(flags, w, out):
    out[...] = w[...].T


def pack_kernel(flags, h_ref, up_ref, neighbours, off, *rest):
    *edges, h, up, sems = rest
    micro, rows, width = h.shape
    copies = [
        pltpu.make_async_copy(h_ref, h, sems.at[0]),
        pltpu.make_async_copy(up_ref, up, sems.at[1]),
    ]
    for copy in copies:
        copy.start()
    nodes = flags[NODES]
    even = flags[EVEN] == 1
    ids = flags[BASE] + lax.broadcasted_iota(jnp.int32, neighbours.shape, 0)
    step = neighbours[...] - ids
    step = jnp.where(step > HALO, step - nodes, step)
    step = jnp.where(step < -HALO, step + nodes, step)
    off[...] = jnp.zeros(off.shape, bf16)
    off[:, :K] = step.astype(f32).astype(bf16)
    for copy in copies:
        copy.wait()
    blank = jnp.zeros((16, width - 512), bf16)

    def edge(upper):
        def cut(value, size):
            return value[rows - size :] if upper else value[:size]

        steps = cut(off, EDGE)
        steps = jnp.concatenate([*[steps[16 * p : 16 * p + 16] for p in range(4)], blank], axis=1)
        inner = [cut(h[m], WIDE) for m in range(micro)] + [steps]
        return jnp.concatenate(inner + [cut(up[m], EDGE) for m in range(micro)], axis=0)

    lower, upper = edge(False), edge(True)
    x, y = jnp.where(even, upper, lower), jnp.where(even, lower, upper)
    edges[0][...] = x
    edges[1][...] = y
    edges[2][...] = y[: edges[2].shape[0]]


def slope(u):
    sig = 1.0 / (1.0 + jnp.exp(-u))
    return sig * (1.0 + u * (1.0 - sig))


def prepare_kernel(active, flags, h, off, w, from_x, from_y, *refs):
    factor, mix, z_out = refs[-3:]
    micro, rows, width = h.shape
    span = rows + 2 * EDGE
    reach = rows + 2 * WIDE
    lanes = -(-reach // 128) * 128

    @pl.when(flags[active] == 1)
    def _():
        even = flags[EVEN] == 1

        def both(start, size):
            x, y = from_x[start : start + size, :], from_y[start : start + size, :]
            return jnp.where(even, y, x), jnp.where(even, x, y)

        low, high = both(micro * WIDE, 16)
        cut = [slice(128 * p, 128 * p + 128) for p in range(EDGE // 16)]
        steps = jnp.concatenate(
            [*[low[:, c] for c in cut], off[...], *[high[:, c] for c in cut]], axis=0
        ).astype(f32)
        column = lax.broadcasted_iota(jnp.int32, (span, lanes), 1).astype(f32)
        row = lax.broadcasted_iota(jnp.int32, (span, lanes), 0).astype(f32)
        distance = column - row - float(HALO)
        count = jnp.zeros((span, lanes), f32)
        for k in range(K):
            count = count + jnp.where(distance == steps[:, k : k + 1], 1.0, 0.0)
        gather = count.astype(bf16)
        mix[...] = (count + jnp.where(distance == 0.0, float(K), 0.0)).T[:reach].astype(bf16)
        blank = jnp.zeros((lanes - reach, width), bf16)
        for m in range(micro):
            low, high = both(m * WIDE, WIDE)
            field = jnp.concatenate([low, h[m], high, blank], axis=0)
            agg = jnp.dot(gather, field, preferred_element_type=f32) * (1.0 / K)
            z_field = (field[HALO : HALO + span].astype(f32) + agg).astype(bf16)
            z_out[m] = z_field[EDGE : EDGE + rows]
            factor[m] = slope(jnp.dot(z_field, w[...], preferred_element_type=f32))


def layer_kernel(layer, m, sources, olds, flags, *refs):
    g_in = refs[:sources]
    factor, mix, w_t = refs[sources : sources + 3]
    grads, kept, *sends = refs[sources + 3 + olds :]
    micro, rows, width = grads.shape
    span = rows + EDGE
    odd = layer % 2 == 1

    @pl.when(flags[layer] == 1)
    def _():
        if layer == 7:
            start = micro * WIDE + 16 + EDGE * m
            x, y = (r[start : start + EDGE, :] for r in g_in[1:])
            own, edge = g_in[0][m], jnp.where(flags[EVEN] == 1, x, y)
        else:
            own, edge = g_in[0][...], g_in[1][...]
        g_field = jnp.concatenate([own, edge] if odd else [edge, own], axis=0)
        first = EDGE if odd else HALO
        du = (g_field.astype(f32) * factor[m, first : first + span, :]).astype(bf16)
        kept[m] = du[EDGE - first : EDGE - first + rows]
        blank = [jnp.zeros((n, width), bf16) for n in (first, mix.shape[1] - span - first)]
        parts = [p for p in (blank[0], du, blank[1]) if p.shape[0]]
        above = WIDE + (HALO if odd else 0)
        mixed = jnp.dot(
            mix[above : above + rows, :], jnp.concatenate(parts, axis=0), preferred_element_type=f32
        )
        mixed = (mixed * (1.0 / K)).astype(bf16)
        dz = jnp.dot(mixed, w_t[...], preferred_element_type=f32)
        total = (g_field[HALO : HALO + rows].astype(f32) + dz).astype(bf16)
        grads[m] = total
        if sends:
            sends[0][...] = total
            sends[1][...] = total[rows - EDGE :] if odd else total[:EDGE]


def rim_kernel(flags, grads, out):
    out[...] = grads[:, grads.shape[1] - HALO :, :]


def shift_kernel(flags, grads, rim, out):
    micro, rows, _ = grads.shape
    odd = flags[1] + flags[3] + flags[5] + flags[7] == 1
    for m in range(micro):
        moved = jnp.concatenate([rim[m], grads[m, : rows - HALO, :]], axis=0)
        out[m] = jnp.where(odd, moved, grads[m])


def split_kernel(flags, z, mine, other):
    micro, rows, width = z.shape
    z_t = z[...].reshape(micro * rows, width).T
    even = flags[EVEN] == 1
    upper = flags[LOWER] == 1
    half = mine.shape[0] // 2
    for y in range(4):
        for x in range(4):
            pair = []
            for q in (8 * y + x, 8 * y + 4 + x):
                a, b = z_t[32 * q : 32 * q + 16], z_t[32 * q + 16 : 32 * q + 32]
                pair.append((jnp.where(even, a, b), jnp.where(even, b, a)))
            place = 16 * (4 * y + x)
            for out, low, high in zip((mine, other), *pair):
                out[place : place + 16, :] = jnp.where(upper, low, high)
                out[half + place : half + place + 16, :] = jnp.where(upper, high, low)


def weight_kernel(flags, za, zb, da, db, far, near):
    micro, rows, width = da.shape
    total = jnp.dot(za[...], da[...].reshape(micro * rows, width), preferred_element_type=f32)
    total = total + jnp.dot(
        zb[...], db[...].reshape(micro * rows, width), preferred_element_type=f32
    )
    total = total.astype(bf16)
    half = total.shape[0] // 2
    far[...] = total[:half].reshape(far.shape)
    near[...] = total[half:].reshape(near.shape)


def sum_kernel(flags, parts, out):
    total = parts[0].astype(f32)
    for i in range(1, parts.shape[0]):
        total = total + parts[i].astype(f32)
    out[...] = total


def add_kernel(flags, parts, other, out):
    total = parts[0].astype(f32)
    for i in range(1, parts.shape[0]):
        total = total + parts[i].astype(f32)
    out[...] = total + other[...]


def shards(acts, upstream, weights, neighbours):
    sections = lax.axis_size("section")
    count = lax.axis_size("space")
    section = lax.axis_index("section")
    shard = lax.axis_index("space")
    rows = neighbours.shape[0]
    width = weights.shape[2]
    micro = upstream.shape[0]
    nodes = rows * count
    h, w = acts[0], weights[0]
    span = rows + 2 * EDGE
    reach = rows + 2 * WIDE
    top = [sections - 1]
    rest = list(range(sections - 1))

    extra = [shard % 2 == 0, section < top[0]]
    extra.append((shard // 8) % 2 == 1)
    extra = jnp.stack([*(e.astype(jnp.int32) for e in extra), shard * rows, jnp.int32(nodes)])
    flags = jnp.concatenate([(section == jnp.arange(sections)).astype(jnp.int32), extra])

    def beside(which, j):
        return (j ^ 1) if which == 0 else (j - 1 if j % 2 == 0 else j + 1) % count

    def edges(which, senders, step):
        return [
            (s * count + j, (s - step) * count + beside(which, j)) for s in senders for j in range(count)
        ]

    def toward(senders, step, side):
        return [(s * count + j, (s - step) * count + (j + side) % count) for s in senders for j in range(count)]

    def swap(bit):
        return [(s * count + j, s * count + (j ^ bit)) for s in range(sections) for j in range(count)]

    short = ((micro * WIDE + 16, width), bf16)
    long = ((micro * (WIDE + EDGE) + 16, width), bf16)
    shapes = [((rows, 128), bf16), long, long, short]
    whole = pl.BlockSpec(memory_space=pltpu.HBM)
    off, from_x, ty, y_pack = pl.pallas_call(
        pack_kernel,
        out_shape=tuple(pltpu.VMEM(shape, dtype) for shape, dtype in shapes),
        in_specs=[SMEM, whole, whole, VMEM],
        out_specs=tuple([VMEM] * len(shapes)),
        scratch_shapes=[
            pltpu.VMEM((micro, rows, width), bf16),
            pltpu.VMEM((micro, rows, width), bf16),
            pltpu.SemaphoreType.DMA((2,)),
        ],
        compiler_params=LIMIT,
        name="pack",
    )(flags, *(pltpu.with_memory_space_constraint(a, pltpu.HBM) for a in (h, upstream)), on_chip(neighbours))
    h, upstream, off = lax.optimization_barrier((h, upstream, off))
    ty = permute(ty, edges(1, top, 0))
    from_x = permute(from_x, swap(1))
    (w_t,) = call(turn_kernel, [((width, width), bf16)], flags, [w])
    w_t, y_pack = lax.optimization_barrier((w_t, y_pack))
    ry = permute(y_pack, edges(1, rest, 0))
    field = ((micro, rows, width), bf16)
    made = [((micro, span, width), f32), ((reach, span), bf16), field]

    def prepare(active, sides, old=()):
        return call(
            functools.partial(prepare_kernel, active),
            made,
            flags,
            [h, off, w, *sides, *old],
            {6 + i: i for i in range(len(old))},
        )

    prepared = prepare(top[0], (from_x, ty))
    grads = kept = None
    received = [[upstream, from_x, ty]] * micro
    for layer in reversed(range(sections)):
        if layer == rest[-1]:
            grads, *prepared = lax.optimization_barrier((grads, *prepared))
            prepared = prepare(REST, (from_x, ry), prepared)
        if layer == rest[-1] - 1:
            half_shape = ((width // 2, micro * rows), bf16)
            grads, z = lax.optimization_barrier((grads, prepared[2]))
            mine, other = call(split_kernel, [half_shape] * 2, flags, [z])
            other = permute(other, swap(1))
            grads, other = lax.optimization_barrier((grads, other))
        factor, mix, _ = prepared
        arriving = []
        for m in range(micro):
            old = [] if grads is None else [grads, kept]
            sent = [((r, width), bf16) for r in (rows, EDGE)] if layer else []
            first = 4 + len(received[m])
            grads, kept, *sends = call(
                functools.partial(layer_kernel, layer, m, len(received[m]), len(old)),
                [field, field, *sent],
                flags,
                [*received[m], factor, mix, w_t, *old],
                {first + i: i for i in range(len(old))},
            )
            if layer:
                side = 1 if layer % 2 else -1
                edge = permute(sends[1], toward([layer], 1, side))
                main = permute(sends[0], toward([layer], 1, 0))
                arriving.append([main, edge])
        received = arriving
        if layer == 1:
            (rim,) = call(rim_kernel, [((micro, HALO, width), bf16)], flags, [grads])
            rim = permute(rim, toward(range(1, sections, 2), 0, 1))

    du_other = permute(kept, swap(1))
    slab = (width // count, width)
    far, close = call(
        weight_kernel, [((16, *slab), bf16)] * 2, flags, [mine, other, kept, du_other]
    )
    groups = [
        [16 * y + 8 * z + 2 * x + c for y in range(4) for x in range(4)]
        for z in range(2)
        for c in range(2)
    ]
    far = lax.all_to_all(far, "space", 0, 0, axis_index_groups=groups)
    close = lax.all_to_all(close, "space", 0, 0, axis_index_groups=groups)
    (far,) = call(sum_kernel, [(slab, f32)], flags, [far])
    other = permute(far, swap(8))
    (weight_grad,) = call(add_kernel, [(slab, f32)], flags, [close, other])
    (grads,) = call(shift_kernel, [field], flags, [grads, rim])
    return (grads[None], weight_grad[None])


def solution(mesh):
    in_specs = (
        P("section", None, "space", None),
        P(None, "space", None),
        P("section", None, None),
        P("space", None),
    )
    out_specs = (P("section", None, "space", None), P("section", "space", None))

    return jax.shard_map(shards, mesh=mesh, in_specs=in_specs, out_specs=out_specs, check_vma=False)
```

```python
import functools

import jax
import jax.numpy as jnp
from jax import lax
from jax.experimental import pallas as pl
from jax.experimental.pallas import tpu as pltpu
from jax.sharding import PartitionSpec as P


K = 6
HALO = 32
EDGE = 2 * HALO
WIDE = 3 * HALO
AXES = ("section", "space")

bf16 = jnp.bfloat16
f32 = jnp.float32
VMEM = pl.BlockSpec(memory_space=pltpu.VMEM)
SMEM = pl.BlockSpec(memory_space=pltpu.SMEM)
LIMIT = pltpu.CompilerParams(vmem_limit_bytes=16 * 1024 * 1024)
EVEN, REST, LOWER, BASE, NODES = 8, 9, 10, 11, 12


def on_chip(value):
    return pltpu.with_memory_space_constraint(value, pltpu.VMEM)


def permute(value, pairs):
    return lax.ppermute(value, AXES, pairs)


def call(kernel, outs, flags, arrays, aliases=None):
    return pl.pallas_call(
        kernel,
        out_shape=tuple(pltpu.VMEM(shape, dtype) for shape, dtype in outs),
        in_specs=[SMEM] + [VMEM] * len(arrays),
        out_specs=tuple([VMEM] * len(outs)),
        input_output_aliases=aliases or {},
        compiler_params=LIMIT,
    )(flags, *[on_chip(a) for a in arrays])


def turn_kernel(flags, w, out):
    out[...] = w[...].T


def pack_kernel(flags, h_ref, up_ref, neighbours, off, *rest):
    *edges, h, up, sems = rest
    micro, rows, width = h.shape
    copies = [
        pltpu.make_async_copy(h_ref, h, sems.at[0]),
        pltpu.make_async_copy(up_ref, up, sems.at[1]),
    ]
    for copy in copies:
        copy.start()
    nodes = flags[NODES]
    even = flags[EVEN] == 1
    ids = flags[BASE] + lax.broadcasted_iota(jnp.int32, neighbours.shape, 0)
    step = neighbours[...] - ids
    step = jnp.where(step > HALO, step - nodes, step)
    step = jnp.where(step < -HALO, step + nodes, step)
    off[...] = jnp.zeros(off.shape, bf16)
    off[:, :K] = step.astype(f32).astype(bf16)
    for copy in copies:
        copy.wait()
    blank = jnp.zeros((16, width - 512), bf16)

    def edge(upper):
        def cut(value, size):
            return value[rows - size :] if upper else value[:size]

        steps = cut(off, EDGE)
        steps = jnp.concatenate([*[steps[16 * p : 16 * p + 16] for p in range(4)], blank], axis=1)
        inner = [cut(h[m], WIDE) for m in range(micro)] + [steps]
        return jnp.concatenate(inner + [cut(up[m], EDGE) for m in range(micro)], axis=0)

    lower, upper = edge(False), edge(True)
    x, y = jnp.where(even, upper, lower), jnp.where(even, lower, upper)
    edges[0][...] = x
    edges[1][...] = y
    edges[2][...] = y[: edges[2].shape[0]]


def slope(u):
    sig = 1.0 / (1.0 + jnp.exp(-u))
    return sig * (1.0 + u * (1.0 - sig))


def prepare_kernel(active, flags, h, off, w, from_x, from_y, *refs):
    factor, mix, z_out = refs[-3:]
    micro, rows, width = h.shape
    span = rows + 2 * EDGE
    reach = rows + 2 * WIDE
    lanes = -(-reach // 128) * 128

    @pl.when(flags[active] == 1)
    def _():
        even = flags[EVEN] == 1

        def both(start, size):
            x, y = from_x[start : start + size, :], from_y[start : start + size, :]
            return jnp.where(even, y, x), jnp.where(even, x, y)

        low, high = both(micro * WIDE, 16)
        cut = [slice(128 * p, 128 * p + 128) for p in range(EDGE // 16)]
        steps = jnp.concatenate(
            [*[low[:, c] for c in cut], off[...], *[high[:, c] for c in cut]], axis=0
        ).astype(f32)
        column = lax.broadcasted_iota(jnp.int32, (span, lanes), 1).astype(f32)
        row = lax.broadcasted_iota(jnp.int32, (span, lanes), 0).astype(f32)
        distance = column - row - float(HALO)
        count = jnp.zeros((span, lanes), f32)
        for k in range(K):
            count = count + jnp.where(distance == steps[:, k : k + 1], 1.0, 0.0)
        gather = count.astype(bf16)
        mix[...] = (count + jnp.where(distance == 0.0, float(K), 0.0)).T[:reach].astype(bf16)
        blank = jnp.zeros((lanes - reach, width), bf16)
        for m in range(micro):
            low, high = both(m * WIDE, WIDE)
            field = jnp.concatenate([low, h[m], high, blank], axis=0)
            agg = jnp.dot(gather, field, preferred_element_type=f32) * (1.0 / K)
            z_field = (field[HALO : HALO + span].astype(f32) + agg).astype(bf16)
            z_out[m] = z_field[EDGE : EDGE + rows]
            factor[m] = slope(jnp.dot(z_field, w[...], preferred_element_type=f32))


def layer_kernel(layer, m, sources, olds, flags, *refs):
    g_in = refs[:sources]
    factor, mix, w_t = refs[sources : sources + 3]
    grads, *sends = refs[sources + 3 + olds :]
    kept = None
    if not (layer == 0 and m == 1):
        kept, *sends = sends
    micro, rows, width = grads.shape
    span = rows + EDGE
    odd = layer % 2 == 1

    @pl.when(flags[layer] == 1)
    def _():
        if layer == 7:
            start = micro * WIDE + 16 + EDGE * m
            x, y = (r[start : start + EDGE, :] for r in g_in[1:])
            own, edge = g_in[0][m], jnp.where(flags[EVEN] == 1, x, y)
        else:
            own, edge = g_in[0][...], g_in[1][...]
        g_field = jnp.concatenate([own, edge] if odd else [edge, own], axis=0)
        first = EDGE if odd else HALO
        du = (g_field.astype(f32) * factor[m, first : first + span, :]).astype(bf16)
        if kept is not None:
            kept[m] = du[EDGE - first : EDGE - first + rows]
        blank = [jnp.zeros((n, width), bf16) for n in (first, mix.shape[1] - span - first)]
        parts = [p for p in (blank[0], du, blank[1]) if p.shape[0]]
        above = WIDE + (HALO if odd else 0)
        mixed = jnp.dot(
            mix[above : above + rows, :], jnp.concatenate(parts, axis=0), preferred_element_type=f32
        )
        mixed = (mixed * (1.0 / K)).astype(bf16)
        dz = jnp.dot(mixed, w_t[...], preferred_element_type=f32)
        total = (g_field[HALO : HALO + rows].astype(f32) + dz).astype(bf16)
        grads[m] = total
        if sends:
            sends[0][...] = total
            sends[1][...] = total[rows - EDGE :] if odd else total[:EDGE]


def last_du_kernel(m, flags, main, edge, factor, old, kept):
    rows = main.shape[0]

    @pl.when(flags[0] == 1)
    def _():
        g_field = jnp.concatenate([edge[EDGE - HALO :, :], main[: rows - HALO, :]], axis=0)
        du = g_field.astype(f32) * factor[m, EDGE : EDGE + rows, :]
        kept[m] = du.astype(bf16)


def rim_kernel(flags, grads, out):
    out[...] = grads[:, grads.shape[1] - HALO :, :]


def shift_kernel(flags, grads, rim, out):
    micro, rows, _ = grads.shape
    odd = flags[1] + flags[3] + flags[5] + flags[7] == 1
    for m in range(micro):
        moved = jnp.concatenate([rim[m], grads[m, : rows - HALO, :]], axis=0)
        out[m] = jnp.where(odd, moved, grads[m])


def split_kernel(flags, z, mine, other):
    micro, rows, width = z.shape
    z_t = z[...].reshape(micro * rows, width).T
    even = flags[EVEN] == 1
    upper = flags[LOWER] == 1
    half = mine.shape[0] // 2
    for y in range(4):
        for x in range(4):
            pair = []
            for q in (8 * y + x, 8 * y + 4 + x):
                a, b = z_t[32 * q : 32 * q + 16], z_t[32 * q + 16 : 32 * q + 32]
                pair.append((jnp.where(even, a, b), jnp.where(even, b, a)))
            place = 16 * (4 * y + x)
            for out, low, high in zip((mine, other), *pair):
                out[place : place + 16, :] = jnp.where(upper, low, high)
                out[half + place : half + place + 16, :] = jnp.where(upper, high, low)


def own_weight_kernel(flags, za, da, out):
    micro, rows, width = da.shape
    out[...] = jnp.dot(za[...], da[...].reshape(micro * rows, width), preferred_element_type=f32)


def weight_kernel(flags, own, zb, db, far, near):
    micro, rows, width = db.shape
    total = own[...] + jnp.dot(
        zb[...], db[...].reshape(micro * rows, width), preferred_element_type=f32
    )
    total = total.astype(bf16)
    half = total.shape[0] // 2
    far[...] = total[:half].reshape(far.shape)
    near[...] = total[half:].reshape(near.shape)


def sum_kernel(flags, parts, out):
    total = parts[0].astype(f32)
    for i in range(1, parts.shape[0]):
        total = total + parts[i].astype(f32)
    out[...] = total


def add_kernel(flags, parts, other, out):
    total = parts[0].astype(f32)
    for i in range(1, parts.shape[0]):
        total = total + parts[i].astype(f32)
    out[...] = total + other[...]


def shards(acts, upstream, weights, neighbours):
    sections = lax.axis_size("section")
    count = lax.axis_size("space")
    section = lax.axis_index("section")
    shard = lax.axis_index("space")
    rows = neighbours.shape[0]
    width = weights.shape[2]
    micro = upstream.shape[0]
    nodes = rows * count
    h, w = acts[0], weights[0]
    span = rows + 2 * EDGE
    reach = rows + 2 * WIDE
    top = [sections - 1]
    rest = list(range(sections - 1))

    extra = [shard % 2 == 0, section < top[0]]
    extra.append((shard // 8) % 2 == 1)
    extra = jnp.stack([*(e.astype(jnp.int32) for e in extra), shard * rows, jnp.int32(nodes)])
    flags = jnp.concatenate([(section == jnp.arange(sections)).astype(jnp.int32), extra])

    def beside(which, j):
        return (j ^ 1) if which == 0 else (j - 1 if j % 2 == 0 else j + 1) % count

    def edges(which, senders, step):
        return [
            (s * count + j, (s - step) * count + beside(which, j)) for s in senders for j in range(count)
        ]

    def toward(senders, step, side):
        return [(s * count + j, (s - step) * count + (j + side) % count) for s in senders for j in range(count)]

    def swap(bit):
        return [(s * count + j, s * count + (j ^ bit)) for s in range(sections) for j in range(count)]

    short = ((micro * WIDE + 16, width), bf16)
    long = ((micro * (WIDE + EDGE) + 16, width), bf16)
    shapes = [((rows, 128), bf16), long, long, short]
    whole = pl.BlockSpec(memory_space=pltpu.HBM)
    off, from_x, ty, y_pack = pl.pallas_call(
        pack_kernel,
        out_shape=tuple(pltpu.VMEM(shape, dtype) for shape, dtype in shapes),
        in_specs=[SMEM, whole, whole, VMEM],
        out_specs=tuple([VMEM] * len(shapes)),
        scratch_shapes=[
            pltpu.VMEM((micro, rows, width), bf16),
            pltpu.VMEM((micro, rows, width), bf16),
            pltpu.SemaphoreType.DMA((2,)),
        ],
        compiler_params=LIMIT,
        name="pack",
    )(flags, *(pltpu.with_memory_space_constraint(a, pltpu.HBM) for a in (h, upstream)), on_chip(neighbours))
    h, upstream, off = lax.optimization_barrier((h, upstream, off))
    ty = permute(ty, edges(1, top, 0))
    from_x = permute(from_x, swap(1))
    (w_t,) = call(turn_kernel, [((width, width), bf16)], flags, [w])
    w_t, y_pack = lax.optimization_barrier((w_t, y_pack))
    ry = permute(y_pack, edges(1, rest, 0))
    field = ((micro, rows, width), bf16)
    made = [((micro, span, width), f32), ((reach, span), bf16), field]

    def prepare(active, sides, old=()):
        return call(
            functools.partial(prepare_kernel, active),
            made,
            flags,
            [h, off, w, *sides, *old],
            {6 + i: i for i in range(len(old))},
        )

    prepared = prepare(top[0], (from_x, ty))
    grads = kept = None
    received = [[upstream, from_x, ty]] * micro
    for layer in reversed(range(sections)):
        if layer == rest[-1]:
            grads, *prepared = lax.optimization_barrier((grads, *prepared))
            prepared = prepare(REST, (from_x, ry), prepared)
        if layer == rest[-1] - 1:
            half_shape = ((width // 2, micro * rows), bf16)
            grads, z = lax.optimization_barrier((grads, prepared[2]))
            mine, other = call(split_kernel, [half_shape] * 2, flags, [z])
            other = permute(other, swap(1))
            grads, other = lax.optimization_barrier((grads, other))
        factor, mix, _ = prepared
        arriving = []
        for m in range(micro):
            last = layer == 0 and m == micro - 1
            if last:
                (kept,) = call(
                    functools.partial(last_du_kernel, m),
                    [field],
                    flags,
                    [*received[m], factor, kept],
                    {4: 0},
                )
                du_other = permute(kept, swap(1))
                (grads,) = call(
                    functools.partial(layer_kernel, layer, m, len(received[m]), 1),
                    [field],
                    flags,
                    [*received[m], factor, mix, w_t, grads],
                    {4 + len(received[m]): 0},
                )
                continue
            old = [] if grads is None else [grads, kept]
            sent = [((r, width), bf16) for r in (rows, EDGE)] if layer else []
            first = 4 + len(received[m])
            grads, kept, *sends = call(
                functools.partial(layer_kernel, layer, m, len(received[m]), len(old)),
                [field, field, *sent],
                flags,
                [*received[m], factor, mix, w_t, *old],
                {first + i: i for i in range(len(old))},
            )
            if layer:
                side = 1 if layer % 2 else -1
                edge = permute(sends[1], toward([layer], 1, side))
                main = permute(sends[0], toward([layer], 1, 0))
                arriving.append([main, edge])
        received = arriving
        if layer == 1:
            (rim,) = call(rim_kernel, [((micro, HALO, width), bf16)], flags, [grads])
            rim = permute(rim, toward(range(1, sections, 2), 0, 1))

    slab = (width // count, width)
    (own,) = call(own_weight_kernel, [((width // 2, width), f32)], flags, [mine, kept])
    far, close = call(weight_kernel, [((16, *slab), bf16)] * 2, flags, [own, other, du_other])
    groups = [
        [16 * y + 8 * z + 2 * x + c for y in range(4) for x in range(4)]
        for z in range(2)
        for c in range(2)
    ]
    far = lax.all_to_all(far, "space", 0, 0, axis_index_groups=groups)
    close = lax.all_to_all(close, "space", 0, 0, axis_index_groups=groups)
    (far,) = call(sum_kernel, [(slab, f32)], flags, [far])
    other = permute(far, swap(8))
    (weight_grad,) = call(add_kernel, [(slab, f32)], flags, [close, other])
    (grads,) = call(shift_kernel, [field], flags, [grads, rim])
    return (grads[None], weight_grad[None])


def solution(mesh):
    in_specs = (
        P("section", None, "space", None),
        P(None, "space", None),
        P("section", None, None),
        P("space", None),
    )
    out_specs = (P("section", None, "space", None), P("section", "space", None))

    return jax.shard_map(shards, mesh=mesh, in_specs=in_specs, out_specs=out_specs, check_vma=False)
```
